32 devices in a mesh: grp: 2 (over y), row: 4 (over x, core), col: 4 (over z).
Axes of the slice: x: 2, y: 2, z: 4, core: 2. Of those that a mesh axis runs over, the one named last changes fastest.
Arguments:
- dosage: float32 [16384, 2048], P(('grp', 'row'), 'col'), parts along dimension 0, as said below
- phenotypes: float32 [16384, 64], P(('grp', 'row'), 'col'), parts along dimension 0, may hold values from -6 to 6
- solution: float32 [4096, 64], P(('grp', 'col')), parts along dimension 0, may hold values from -6 to 6
- inverse_factor: float32 [4096, 2048], P(('grp', 'col'), 'row'), parts along dimension 0, as said below
Outputs:
- residual: float32 [16384, 64], P(('grp', 'row'), 'col'), parts along dimension 0
- correction: float32 [4096, 64], P(('grp', 'col')), parts along dimension 0
The draws below stay inside these ranges and needn't reach their ends.
There are 2 independent parts, one for each index of `grp`. The reference program is written for one: setup_inputs(seed, part) draws one part's arguments, and reference() takes and returns one part's arrays. A program takes and returns all parts, laid end to end along the dimension named above; each array names one. Nothing has to cross between parts.
Inputs may be any that keep to these rules, and one draw needn't show every extreme that they name: `dosage`: dense real-valued entries. `inverse_factor`: upper triangular: entries below the diagonal are zero, diagonal entries positive; a given preconditioner, not derived from the slab's values.
All inputs are finite; a program needn't handle non-finite values.
Results may differ from the reference program's by a relative error of at most 0.00013.
Values sent between devices are 32-bit elements; how exact they have to be, the bound alone decides.
A program may use at most 64 MiB of HBM per device.

```python
import jax
import jax.numpy as jnp
from jax import lax

N = 2048
P_SIZE = 64
ITERS = 2
ROWS = 8192


def draw_dosage(key, part):
    key_base = jax.random.fold_in(jax.random.fold_in(key, 11), 0)
    base = jax.random.normal(key_base, (ROWS, N), jnp.float32)
    return base / jnp.sqrt(jnp.float32(ROWS))


def draw_inverse_factor(key, part):
    key_diag, key_off = jax.random.split(jax.random.fold_in(key, 23), 2)
    row_ids = lax.broadcasted_iota(jnp.int32, (N, N), 0)
    col_ids = lax.broadcasted_iota(jnp.int32, (N, N), 1)
    diagonal = jax.random.uniform(key_diag, (N, 1), jnp.float32, 0.5, 0.9)
    above = jax.random.normal(key_off, (N, N), jnp.float32)
    above = above * (0.3 / jnp.sqrt(jnp.float32(N)))
    zeros = jnp.zeros((N, N), jnp.float32)
    return jnp.where(col_ids > row_ids, above, jnp.where(col_ids == row_ids, diagonal, zeros))


def shard_levels(key, shape, cuts, smallest, largest):
    factor_of = 1.0
    for dim, blocks in cuts:
        steps = jax.random.uniform(jax.random.fold_in(jax.random.fold_in(key, 6), dim), (blocks,), jnp.float32, smallest / len(cuts), largest / len(cuts))
        factor_of = factor_of * jnp.repeat(jnp.exp(steps), shape[dim] // blocks).reshape((-1,) + (1,) * (len(shape) - 1 - dim))
    return factor_of


def bell_draw(rng, extent, width, reach, cuts=(), held_as=jnp.bfloat16):
    entries = width * jax.random.normal(rng, extent, jnp.float32)
    if cuts:
        entries = entries * shard_levels(rng, extent, cuts, -0.22, 0.18)
    return jnp.clip(entries, -reach, reach).astype(held_as)


def setup_inputs(seed: int = 0, part: int = 0) -> dict:
    keys = jax.random.split(jax.random.key(seed), 5)
    own_keys = jax.random.split(jax.random.fold_in(keys[4], part), 5)
    return {
        "dosage": draw_dosage(jax.random.fold_in(jax.random.fold_in(keys[4], part), 71), part),
        "phenotypes": bell_draw(own_keys[1], (ROWS, P_SIZE), 1.0, 6.0, ((0, 4), (1, 4)), jnp.float32),
        "solution": bell_draw(own_keys[2], (N, P_SIZE), 1.0, 6.0, ((0, 4),), jnp.float32),
        "inverse_factor": draw_inverse_factor(jax.random.fold_in(jax.random.fold_in(keys[4], part), 71), part),
    }


def reference(dosage, phenotypes, solution, inverse_factor):
    precise = lax.Precision.HIGHEST
    field = solution
    correction = jnp.zeros_like(solution)
    for step in range(ITERS):
        resid = phenotypes - jnp.dot(dosage, field, precision=precise, preferred_element_type=jnp.float32)
        side = jnp.dot(dosage.T, resid, precision=precise, preferred_element_type=jnp.float32)
        inner = jnp.dot(inverse_factor.T, side, precision=precise, preferred_element_type=jnp.float32)
        change = jnp.dot(inverse_factor, inner, precision=precise, preferred_element_type=jnp.float32)
        field = field + change
        correction = correction + change
    residual = phenotypes - jnp.dot(dosage, field, precision=precise, preferred_element_type=jnp.float32)
    return residual, correction
```

```python
import functools

import jax
import jax.numpy as jnp
from jax import lax
from jax.experimental import pallas as pl
from jax.experimental.pallas import tpu as pltpu
from jax.sharding import PartitionSpec as P

ITERS = 2
MESH = pl.DeviceIdType.MESH
F32 = jnp.float32
BF16 = jnp.bfloat16
NN = (((1,), (0,)), ((), ()))
NT = (((1,), (1,)), ((), ()))


def split(value):
    high = value.astype(BF16)
    low = (value - high.astype(F32)).astype(BF16)
    return high, low


def product(left, right_high, right_low, dims):
    count = left.shape[0] // 2
    main = lax.dot_general(left, right_high, dims, preferred_element_type=F32)
    rest = lax.dot_general(left[:count], right_low, dims, preferred_element_type=F32)
    return main[:count] + (main[count:] + rest)


def stacked(value):
    return jnp.concatenate(split(value), axis=0)


def kernel(cfg, dosage, pheno, start, factor, residual, correction, *scratch):
    (n_row, n_col, chunks, n_in) = cfg
    (d_f32, d_hi, d_lo, y_in, y_pad, f_in, field, r_f32, r_hi, r_lo,
     own, got_p, got_s, put_p, put_s,
     f_own, f_got_p, f_got_s, f_put_p, f_put_s,
     acc, pair_got, cross_put, cross_got, back_put, back_got,
     i_own, i_got_p, i_got_s, i_put_p, i_put_s, inner,
     load_sem, d_sem, a_sem, f_sem, pair_sem, cross_ssem, cross_rsem, i_sem) = scratch
    rows_c = d_hi.shape[1]
    n_p = field.shape[0]
    half = n_p // 2
    blk = pheno.shape[0]
    n_half = f_own.shape[1]
    width = f_own.shape[3]
    n_x = n_row // 2

    row = lax.axis_index("row")
    col = lax.axis_index("col")
    core = lax.rem(row, 2)
    x = row // 2
    partner = {"row": row + 1 - 2 * core}
    is_first = col == 0
    is_last = col == n_col - 1

    loads = []
    for k, (src, dst) in enumerate(((start, f_in), (pheno, y_in), (factor, r_f32))):
        loads.append(pltpu.make_async_copy(src, dst, load_sem.at[k]))

    def d_copy(c):
        return pltpu.make_async_copy(
            dosage.at[pl.ds(pl.multiple_of(c * rows_c, rows_c), rows_c), :], d_f32.at[c], d_sem.at[c])

    loads[0].start()
    loads[1].start()
    for c in range(chunks):
        d_copy(c).start()
    loads[2].start()

    barrier = pltpu.get_barrier_semaphore()

    @pl.when(col > 0)
    def _():
        pl.semaphore_signal(barrier, inc=1, device_id={"col": col - 1}, device_id_type=MESH)

    @pl.when(col < n_col - 1)
    def _():
        pl.semaphore_signal(barrier, inc=1, device_id={"col": col + 1}, device_id_type=MESH)

    pl.semaphore_signal(barrier, inc=1, device_id=partner, device_id_type=MESH)
    for d in range(1, n_x):
        other = lax.rem(x + d, n_x) * 2 + core
        pl.semaphore_signal(barrier, inc=1, device_id={"row": other}, device_id_type=MESH)

    loads[0].wait()
    loads[1].wait()
    field[...] = f_in[...]
    for c in range(chunks):
        y_c = y_in[:, c * rows_c:(c + 1) * rows_c]
        for b in range(n_col):
            y_pad[c, b * blk:(b + 1) * blk, :] = jnp.where(col == b, y_c, 0.0)

    up_down = jnp.where(is_first, 0, 1) + jnp.where(is_last, 0, 1)
    pl.semaphore_wait(barrier, n_x + up_down)

    def line(src, dst, sems, way, c, step):
        return pltpu.make_async_remote_copy(
            src_ref=src, dst_ref=dst, send_sem=sems.at[way, 0, c], recv_sem=sems.at[way, 1, c],
            device_id={"col": jnp.clip(col + step, 0, n_col - 1)}, device_id_type=MESH)

    def fit(c, f_cat):
        return product(f_cat, d_hi[c], d_lo[c], NT) - y_pad[c]

    def up(it, c, src):
        return line(src, got_p.at[it, c], a_sem.at[it], 0, c, 1)

    def down(it, c, src):
        return line(src, got_s.at[it, c], a_sem.at[it], 1, c, -1)

    def fit_and_sum(it):
        f_cat = stacked(field[...])

        def make(c, carry):
            if it == 0:
                d_copy(c).wait()
                high, low = split(d_f32[c])
                d_hi[c] = high
                d_lo[c] = low
            own[it, c] = fit(c, f_cat)

            @pl.when(is_first)
            def _():
                up(it, c, own.at[it, c]).start()

            @pl.when(is_last)
            def _():
                down(it, c, own.at[it, c]).start()
            return carry

        lax.fori_loop(0, chunks, make, 0)
        acc[...] = jnp.zeros_like(acc)
        middle = jnp.logical_and(col > 0, col < n_col - 1)
        lag = jnp.where(middle, 2 * (n_col - 1 - 2 * col), 0)
        lag_s = jnp.clip(lag, 0, chunks)
        lag_p = jnp.clip(-lag, 0, chunks)
        lag_max = min(chunks, 2 * max(n_col - 3, 0))

        def step(i, carry):
            c_p = i - lag_p
            c_s = i - lag_s

            @pl.when(jnp.logical_and(jnp.logical_and(c_p >= 0, c_p < chunks), col > 0))
            def _():
                up(it, c_p, own.at[it, c_p]).wait_recv()

                @pl.when(col < n_col - 1)
                def _():
                    put_p[it, c_p] = got_p[it, c_p] + own[it, c_p]
                    up(it, c_p, put_p.at[it, c_p]).start()

            @pl.when(jnp.logical_and(jnp.logical_and(c_s >= 0, c_s < chunks), col < n_col - 1))
            def _():
                down(it, c_s, own.at[it, c_s]).wait_recv()

                @pl.when(col > 0)
                def _():
                    put_s[it, c_s] = got_s[it, c_s] + own[it, c_s]
                    down(it, c_s, put_s.at[it, c_s]).start()

            c = i - lag_p - lag_s

            @pl.when(jnp.logical_and(c >= 0, c < chunks))
            def _():
                before = jnp.where(is_first, 0.0, got_p[it, c])
                after = jnp.where(is_last, 0.0, got_s[it, c])
                resid = before + own[it, c] + after
                acc[...] += product(stacked(resid), d_hi[c], d_lo[c], NN)
            return carry

        lax.fori_loop(0, chunks + lag_max, step, 0)

    def drain_sum(it):
        def step(c, carry):
            @pl.when(col < n_col - 1)
            def _():
                up(it, c, own.at[it, c]).wait_send()

            @pl.when(col > 0)
            def _():
                down(it, c, own.at[it, c]).wait_send()
            return carry

        lax.fori_loop(0, chunks, step, 0)

    def row_sum(k):
        for h in range(2):
            back_put[k, h] = acc[h * half:(h + 1) * half, :]
        first = pltpu.make_async_remote_copy(
            src_ref=back_put.at[k, 1 - core], dst_ref=pair_got.at[k],
            send_sem=pair_sem.at[k, 0], recv_sem=pair_sem.at[k, 1],
            device_id=partner, device_id_type=MESH)
        first.start()
        first.wait_recv()
        cross_put[k] = back_put[k, core] + pair_got[k]
        sends = []
        for d in range(1, n_x):
            other = lax.rem(x + d, n_x) * 2 + core
            sends.append(pltpu.make_async_remote_copy(
                src_ref=cross_put.at[k], dst_ref=cross_got.at[k, d - 1],
                send_sem=cross_ssem.at[k, d - 1], recv_sem=cross_rsem.at[k, d - 1],
                device_id={"row": other}, device_id_type=MESH))
            sends[-1].start()
        parts = [cross_put[k]]
        for d in range(1, n_x):
            sends[d - 1].wait_recv()
            parts.append(cross_got[k, d - 1])
        total = None
        for chip in range(n_x):
            here = parts[0]
            for d in range(1, n_x):
                here = jnp.where(lax.rem(x - d + n_x, n_x) == chip, parts[d], here)
            total = here if total is None else total + here
        back_got[k, 2] = total
        last = pltpu.make_async_remote_copy(
            src_ref=back_got.at[k, 2], dst_ref=back_got.at[k, core],
            send_sem=pair_sem.at[k, 2], recv_sem=pair_sem.at[k, 3],
            device_id=partner, device_id_type=MESH)
        last.start()
        last.wait_recv()
        theirs = back_got[k, 1 - core]
        mine = total
        low = jnp.where(core == 0, mine, theirs)
        high = jnp.where(core == 0, theirs, mine)
        acc[0:half, :] = low
        acc[half:, :] = high
        for copy in (first, last, *sends):
            copy.wait_send()

    n_rb = r_hi.shape[1]
    n_cb = r_hi.shape[0]
    active_last = ((row + 1) * n_rb + n_cb - 1) // n_cb - 1
    active_last = jnp.minimum(active_last, n_col - 1)
    wide_i = n_p // n_in

    def i_up(it, c, src):
        return line(src, i_got_p.at[it, c], i_sem.at[it], 0, c, 1)

    def i_down(it, c, src):
        return line(src, i_got_s.at[it, c], i_sem.at[it], 1, c, -1)

    def solve(it):
        if it == 0:
            loads[2].wait()
            high, low = split(r_f32[...])
            r_hi[...] = high
            r_lo[...] = low

        @pl.when(col <= active_last)
        def _():
            part = product(stacked(acc[...]), r_hi[...], r_lo[...], NN)
            for c in range(n_in):
                i_own[it, c] = part[c * wide_i:(c + 1) * wide_i]

            @pl.when(jnp.logical_and(is_first, active_last > 0))
            def _():
                for c in range(n_in):
                    i_up(it, c, i_own.at[it, c]).start()

            @pl.when(jnp.logical_and(col == active_last, active_last > 0))
            def _():
                for c in range(n_in):
                    i_down(it, c, i_own.at[it, c]).start()

            lag = jnp.where(jnp.logical_and(col > 0, col < active_last), 2 * (active_last - 2 * col), 0)
            lag_s = jnp.clip(lag, 0, n_in)
            lag_p = jnp.clip(-lag, 0, n_in)
            lag_max = min(n_in, 2 * max(n_col - 3, 0))

            def step(i, carry):
                c_p = i - lag_p
                c_s = i - lag_s

                @pl.when(jnp.logical_and(jnp.logical_and(c_p >= 0, c_p < n_in), col > 0))
                def _():
                    i_up(it, c_p, i_own.at[it, c_p]).wait_recv()

                    @pl.when(col < active_last)
                    def _():
                        i_put_p[it, c_p] = i_got_p[it, c_p] + i_own[it, c_p]
                        i_up(it, c_p, i_put_p.at[it, c_p]).start()

                @pl.when(jnp.logical_and(jnp.logical_and(c_s >= 0, c_s < n_in), col < active_last))
                def _():
                    i_down(it, c_s, i_own.at[it, c_s]).wait_recv()

                    @pl.when(col > 0)
                    def _():
                        i_put_s[it, c_s] = i_got_s[it, c_s] + i_own[it, c_s]
                        i_down(it, c_s, i_put_s.at[it, c_s]).start()
                return carry

            lax.fori_loop(0, n_in + lag_max, step, 0)
            for c in range(n_in):
                before = jnp.where(is_first, 0.0, i_got_p[it, c])
                after = jnp.where(col == active_last, 0.0, i_got_s[it, c])
                inner[c * wide_i:(c + 1) * wide_i, :] = before + i_own[it, c] + after
            acc[...] = product(stacked(inner[...]), r_hi[...], r_lo[...], NT)

        @pl.when(col > active_last)
        def _():
            acc[...] = jnp.zeros_like(acc)

    def drain_solve(it):
        for c in range(n_in):
            @pl.when(col < active_last)
            def _():
                i_up(it, c, i_own.at[it, c]).wait_send()

            @pl.when(jnp.logical_and(col > 0, col <= active_last))
            def _():
                i_down(it, c, i_own.at[it, c]).wait_send()

    def f_up(q, src):
        b = n_col - 1 - q // n_half
        return line(src, f_got_p.at[b, lax.rem(q, n_half)], f_sem, 0, q, 1)

    def f_down(q, src):
        b = q // n_half
        return line(src, f_got_s.at[b, lax.rem(q, n_half)], f_sem, 1, q, -1)

    def finish():
        f_cat = stacked(field[...])
        per = width // rows_c
        for c in range(chunks):
            value = fit(c, f_cat)
            for b in range(n_col):
                f_own[b, c // per, :, (c % per) * rows_c:(c % per + 1) * rows_c] = value[b * blk:(b + 1) * blk, :]
        total_q = n_col * n_half

        @pl.when(is_first)
        def _():
            def send(q, carry):
                f_up(q, f_own.at[n_col - 1 - q // n_half, lax.rem(q, n_half)]).start()
                return carry
            lax.fori_loop(0, total_q - n_half, send, 0)

        @pl.when(is_last)
        def _():
            def send(q, carry):
                f_down(q, f_own.at[q // n_half, lax.rem(q, n_half)]).start()
                return carry
            lax.fori_loop(0, total_q - n_half, send, 0)

        middle = jnp.logical_and(col > 0, col < n_col - 1)
        lag = jnp.where(middle, 2 * (n_col - 1 - 2 * col), 0)
        lag_s = jnp.clip(lag, 0, total_q)
        lag_p = jnp.clip(-lag, 0, total_q)
        lag_max = min(total_q, 2 * max(n_col - 3, 0))

        def step(i, carry):
            q_p = i - lag_p
            q_s = i - lag_s
            b_p = n_col - 1 - q_p // n_half
            h_p = lax.rem(q_p, n_half)
            b_s = q_s // n_half
            h_s = lax.rem(q_s, n_half)

            @pl.when(jnp.logical_and(jnp.logical_and(q_p >= 0, q_p < total_q - col * n_half), col > 0))
            def _():
                f_up(q_p, f_own.at[b_p, h_p]).wait_recv()

                @pl.when(b_p > col)
                def _():
                    f_put_p[b_p, h_p] = f_got_p[b_p, h_p] + f_own[b_p, h_p]
                    f_up(q_p, f_put_p.at[b_p, h_p]).start()

            @pl.when(jnp.logical_and(jnp.logical_and(q_s >= 0, q_s < (col + 1) * n_half), col < n_col - 1))
            def _():
                f_down(q_s, f_own.at[b_s, h_s]).wait_recv()

                @pl.when(b_s < col)
                def _():
                    f_put_s[b_s, h_s] = f_got_s[b_s, h_s] + f_own[b_s, h_s]
                    f_down(q_s, f_put_s.at[b_s, h_s]).start()
            return carry

        lax.fori_loop(0, total_q + lag_max, step, 0)
        for h in range(n_half):
            before = jnp.where(is_first, 0.0, f_got_p[col, h])
            after = jnp.where(is_last, 0.0, f_got_s[col, h])
            residual[:, h * width:(h + 1) * width] = -(before + f_own[col, h] + after)

        def drain(q, carry):
            @pl.when(q < (n_col - 1 - col) * n_half)
            def _():
                f_up(q, f_own.at[0, 0]).wait_send()

            @pl.when(q < col * n_half)
            def _():
                f_down(q, f_own.at[0, 0]).wait_send()
            return carry

        lax.fori_loop(0, total_q, drain, 0)

    for it in range(ITERS):
        fit_and_sum(it)
        row_sum(2 * it)
        solve(it)
        row_sum(2 * it + 1)
        field[...] = field[...] - acc[...]
        if it == 0:
            correction[...] = -acc[...]
        else:
            correction[...] = correction[...] - acc[...]
    finish()
    for it in range(ITERS):
        drain_sum(it)
        drain_solve(it)


def local(n_row, n_col, dosage, phenotypes, solution, inverse_factor):
    rows, cols = dosage.shape
    blk = phenotypes.shape[1]
    n_p = solution.shape[1]
    n_rb = inverse_factor.shape[1]
    chunks = 8
    rows_c = rows // chunks
    n_in = 4
    n_half = 2
    n_x = n_row // 2
    big = pltpu.VMEM((ITERS, chunks, n_p, rows_c), F32)
    last = pltpu.VMEM((n_col, n_half, blk, rows // n_half), F32)
    mid = pltpu.VMEM((ITERS, n_in, n_p // n_in, n_rb), F32)
    k = 2 * ITERS
    scratch = [
        pltpu.VMEM((chunks, rows_c, cols), F32),
        pltpu.VMEM((chunks, rows_c, cols), BF16),
        pltpu.VMEM((chunks, rows_c, cols), BF16),
        pltpu.VMEM((blk, rows), F32),
        pltpu.VMEM((chunks, n_p, rows_c), F32),
        pltpu.VMEM((n_p, cols), F32),
        pltpu.VMEM((n_p, cols), F32),
        pltpu.VMEM(inverse_factor.shape, F32),
        pltpu.VMEM(inverse_factor.shape, BF16),
        pltpu.VMEM(inverse_factor.shape, BF16),
        big, big, big, big, big,
        last, last, last, last, last,
        pltpu.VMEM((n_p, cols), F32),
        pltpu.VMEM((k, n_p // 2, cols), F32),
        pltpu.VMEM((k, n_p // 2, cols), F32),
        pltpu.VMEM((k, max(n_x - 1, 1), n_p // 2, cols), F32),
        pltpu.VMEM((k, 2, n_p // 2, cols), F32),
        pltpu.VMEM((k, 3, n_p // 2, cols), F32),
        mid, mid, mid, mid, mid,
        pltpu.VMEM((n_p, n_rb), F32),
        pltpu.SemaphoreType.DMA((3,)),
        pltpu.SemaphoreType.DMA((chunks,)),
        pltpu.SemaphoreType.DMA((ITERS, 2, 2, chunks)),
        pltpu.SemaphoreType.DMA((2, 2, n_col * n_half)),
        pltpu.SemaphoreType.DMA((k, 4)),
        pltpu.SemaphoreType.DMA((k, max(n_x - 1, 1))),
        pltpu.SemaphoreType.DMA((k, max(n_x - 1, 1))),
        pltpu.SemaphoreType.DMA((ITERS, 2, 2, n_in)),
    ]
    any_spec = pl.BlockSpec(memory_space=pl.ANY)
    vmem_spec = pl.BlockSpec(memory_space=pltpu.VMEM)
    residual, correction = pl.pallas_call(
        functools.partial(kernel, (n_row, n_col, chunks, n_in)),
        out_shape=(
            jax.ShapeDtypeStruct((blk, rows), F32),
            jax.ShapeDtypeStruct((n_p, cols), F32),
        ),
        in_specs=[any_spec] * 4,
        out_specs=(vmem_spec, vmem_spec),
        scratch_shapes=scratch,
        compiler_params=pltpu.CompilerParams(collective_id=0, has_side_effects=True),
    )(dosage, phenotypes.T, solution.T, inverse_factor)
    return residual.T, correction.T


def solution(mesh):
    return jax.shard_map(
        functools.partial(local, mesh.shape["row"], mesh.shape["col"]),
        mesh=mesh,
        in_specs=(
            P(("grp", "row"), "col"),
            P(("grp", "row"), "col"),
            P(("grp", "col"), None),
            P(("grp", "col"), "row"),
        ),
        out_specs=(P(("grp", "row"), "col"), P(("grp", "col"), None)),
        check_vma=False,
    )
```

```python
import functools

import jax
import jax.numpy as jnp
from jax import lax
from jax.experimental import pallas as pl
from jax.experimental.pallas import tpu as pltpu
from jax.sharding import PartitionSpec as P

ITERS = 2
MESH = pl.DeviceIdType.MESH
F32 = jnp.float32
BF16 = jnp.bfloat16
COST_FIT = 0.25
COST_STEP = 0.3
PITCH = 0.5
NN = (((1,), (0,)), ((), ()))
NT = (((1,), (1,)), ((), ()))


def split(value):
    high = value.astype(BF16)
    low = (value - high.astype(F32)).astype(BF16)
    return high, low


def product(left, right_high, right_low, dims):
    count = left.shape[0] // 2
    main = lax.dot_general(left, right_high, dims, preferred_element_type=F32)
    rest = lax.dot_general(left[:count], right_low, dims, preferred_element_type=F32)
    return main[:count] + (main[count:] + rest)


def stacked(value):
    return jnp.concatenate(split(value), axis=0)


def kernel(cfg, dosage, pheno, start, factor, residual, correction, *scratch):
    (n_row, n_col, streams, chunks, n_in, lag, lag_in, lag_f) = cfg
    (d_f32, d_hi, d_lo, y_in, y_pad, f_in, field, total_change, r_f32, r_hi, r_lo,
     own, got_p, got_s, put_p, put_s,
     f_own, f_got_p, f_got_s, f_put_p, f_put_s,
     acc, pair_got, cross_put, cross_got, back_put, back_got,
     i_own, i_got_p, i_got_s, i_put_p, i_put_s,
     load_sem, d_sem, a_sem, f_sem, pair_sem, cross_ssem, cross_rsem, i_sem) = scratch
    rows_c = d_hi.shape[1]
    n_p = field.shape[1]
    half = n_p // 2
    blk = pheno.shape[0]
    sub = blk // streams
    n_half = f_own.shape[2]
    width = f_own.shape[4]
    n_x = n_row // 2

    row = lax.axis_index("row")
    col = lax.axis_index("col")
    core = lax.rem(row, 2)
    x = row // 2
    partner = {"row": row + 1 - 2 * core}
    is_first = col == 0
    is_last = col == n_col - 1

    loads = []
    for k, (src, dst) in enumerate(((start, f_in), (pheno, y_in), (factor, r_f32))):
        loads.append(pltpu.make_async_copy(src, dst, load_sem.at[k]))

    def d_copy(c):
        return pltpu.make_async_copy(
            dosage.at[pl.ds(c * rows_c, rows_c), :], d_f32.at[c], d_sem.at[c])

    barrier = pltpu.get_barrier_semaphore()

    @pl.when(col > 0)
    def _():
        pl.semaphore_signal(barrier, inc=1, device_id={"col": col - 1}, device_id_type=MESH)

    @pl.when(col < n_col - 1)
    def _():
        pl.semaphore_signal(barrier, inc=1, device_id={"col": col + 1}, device_id_type=MESH)

    pl.semaphore_signal(barrier, inc=1, device_id=partner, device_id_type=MESH)
    for d in range(1, n_x):
        other = lax.rem(x + d, n_x) * 2 + core
        pl.semaphore_signal(barrier, inc=1, device_id={"row": other}, device_id_type=MESH)

    loads[0].start()
    loads[1].start()
    for c in range(chunks):
        d_copy(c).start()
    loads[2].start()

    def enter():
        up_down = jnp.where(is_first, 0, 1) + jnp.where(is_last, 0, 1)
        pl.semaphore_wait(barrier, n_x + up_down)

    loads[0].wait()
    for s in range(streams):
        for b in range(n_col):
            at = b * blk + s * sub
            field[s, b * sub:(b + 1) * sub, :] = f_in[at:at + sub, :]
    loads[1].wait()
    for s in range(streams):
        for c in range(chunks):
            y_c = y_in[s * sub:(s + 1) * sub, c * rows_c:(c + 1) * rows_c]
            for b in range(n_col):
                y_pad[s, c, b * sub:(b + 1) * sub, :] = jnp.where(col == b, y_c, 0.0)

    def line(src, dst, sems, way, c, step):
        return pltpu.make_async_remote_copy(
            src_ref=src, dst_ref=dst, send_sem=sems.at[way, 0, c], recv_sem=sems.at[way, 1, c],
            device_id={"col": jnp.clip(col + step, 0, n_col - 1)}, device_id_type=MESH)

    def within(value, low, high):
        return jnp.logical_and(value >= low, value < high)

    done = set()

    def fit(s, c, f_cat):
        if c not in done:
            done.add(c)
            d_copy(c).wait()
            high, low = split(d_f32[c])
            d_hi[c] = high
            d_lo[c] = low
        return product(f_cat, d_hi[c], d_lo[c], NT) - y_pad[s, c]

    def up(s, it, c, src):
        return line(src, got_p.at[it, s, c], a_sem.at[it, s], 0, c, 1)

    def down(s, it, c, src):
        return line(src, got_s.at[it, s, c], a_sem.at[it, s], 1, c, -1)

    def fit_and_sum(s, it):
        f_cat = stacked(field[s])
        for c in range(chunks):
            own[it, s, c] = fit(s, c, f_cat)
            if "enter" not in done:
                done.add("enter")
                enter()

            @pl.when(is_first)
            def _():
                up(s, it, c, own.at[it, s, c]).start()

            @pl.when(is_last)
            def _():
                down(s, it, c, own.at[it, s, c]).start()
            yield COST_FIT, (0.0 if c < chunks - 1 else 2.4 - chunks * COST_FIT)
        acc[s] = jnp.zeros_like(acc[s])
        lag_p = lag * (col - 1)
        lag_s = lag * (n_col - 2 - col)
        steps = chunks + lag * (n_col - 2)
        for i in range(steps):
            c_p = i - lag_p
            c_s = i - lag_s

            @pl.when(jnp.logical_and(within(c_p, 0, chunks), col > 0))
            def _():
                up(s, it, c_p, own.at[it, s, c_p]).wait_recv()

                @pl.when(col < n_col - 1)
                def _():
                    put_p[it, s, c_p] = got_p[it, s, c_p] + own[it, s, c_p]
                    up(s, it, c_p, put_p.at[it, s, c_p]).start()

            @pl.when(jnp.logical_and(within(c_s, 0, chunks), col < n_col - 1))
            def _():
                down(s, it, c_s, own.at[it, s, c_s]).wait_recv()

                @pl.when(col > 0)
                def _():
                    put_s[it, s, c_s] = got_s[it, s, c_s] + own[it, s, c_s]
                    down(s, it, c_s, put_s.at[it, s, c_s]).start()

            c = jnp.minimum(jnp.where(is_first, chunks + steps, c_p), jnp.where(is_last, chunks + steps, c_s))

            @pl.when(within(c, 0, chunks))
            def _():
                before = jnp.where(is_first, 0.0, got_p[it, s, c])
                after = jnp.where(is_last, 0.0, got_s[it, s, c])
                resid = before + own[it, s, c] + after
                acc[s] += product(stacked(resid), d_hi[c], d_lo[c], NN)
            yield COST_STEP, PITCH

    def drain_sum(s, it):
        def step(c, carry):
            @pl.when(col < n_col - 1)
            def _():
                up(s, it, c, own.at[it, s, c]).wait_send()

            @pl.when(col > 0)
            def _():
                down(s, it, c, own.at[it, s, c]).wait_send()
            return carry

        lax.fori_loop(0, chunks, step, 0)

    sent = []

    def row_sum(s, k):
        for h in range(2):
            back_put[k, s, h] = acc[s, h * half:(h + 1) * half, :]
        first = pltpu.make_async_remote_copy(
            src_ref=back_put.at[k, s, 1 - core], dst_ref=pair_got.at[k, s],
            send_sem=pair_sem.at[k, s, 0], recv_sem=pair_sem.at[k, s, 1],
            device_id=partner, device_id_type=MESH)
        first.start()
        yield 0.2, 1.0
        first.wait_recv()
        cross_put[k, s] = back_put[k, s, core] + pair_got[k, s]
        sends = []
        for d in range(1, n_x):
            other = lax.rem(x + d, n_x) * 2 + core
            sends.append(pltpu.make_async_remote_copy(
                src_ref=cross_put.at[k, s], dst_ref=cross_got.at[k, s, d - 1],
                send_sem=cross_ssem.at[k, s, d - 1], recv_sem=cross_rsem.at[k, s, d - 1],
                device_id={"row": other}, device_id_type=MESH))
            sends[-1].start()
        yield 0.1, 2.4
        parts = [cross_put[k, s]]
        for d in range(1, n_x):
            sends[d - 1].wait_recv()
            parts.append(cross_got[k, s, d - 1])
        total = None
        for chip in range(n_x):
            here = parts[0]
            for d in range(1, n_x):
                here = jnp.where(lax.rem(x - d + n_x, n_x) == chip, parts[d], here)
            total = here if total is None else total + here
        back_got[k, s, 2] = total
        last = pltpu.make_async_remote_copy(
            src_ref=back_got.at[k, s, 2], dst_ref=back_got.at[k, s, core],
            send_sem=pair_sem.at[k, s, 2], recv_sem=pair_sem.at[k, s, 3],
            device_id=partner, device_id_type=MESH)
        last.start()
        yield 0.1, 1.0
        last.wait_recv()
        theirs = back_got[k, s, 1 - core]
        mine = back_got[k, s, 2]
        acc[s, 0:half, :] = jnp.where(core == 0, mine, theirs)
        acc[s, half:, :] = jnp.where(core == 0, theirs, mine)
        sent.extend((first, last, *sends))

    n_rb = r_hi.shape[1]
    n_cb = r_hi.shape[0]
    active_last = jnp.minimum(((row + 1) * n_rb + n_cb - 1) // n_cb - 1, n_col - 1)
    wide_i = n_p // n_in

    def i_up(s, it, c, src):
        return line(src, i_got_p.at[it, s, c], i_sem.at[it, s], 0, c, 1)

    def i_down(s, it, c, src):
        return line(src, i_got_s.at[it, s, c], i_sem.at[it, s], 1, c, -1)

    def solve(s, it):
        if "factor" not in done:
            done.add("factor")
            loads[2].wait()
            high, low = split(r_f32[...])
            r_hi[...] = high
            r_lo[...] = low

        @pl.when(col <= active_last)
        def _():
            part = product(stacked(acc[s]), r_hi[...], r_lo[...], NN)
            for c in range(n_in):
                i_own[it, s, c] = part[c * wide_i:(c + 1) * wide_i]

            @pl.when(jnp.logical_and(is_first, active_last > 0))
            def _():
                for c in range(n_in):
                    i_up(s, it, c, i_own.at[it, s, c]).start()

            @pl.when(jnp.logical_and(col == active_last, active_last > 0))
            def _():
                for c in range(n_in):
                    i_down(s, it, c, i_own.at[it, s, c]).start()
        yield 0.4, 2.2
        lag_p = lag_in * (col - 1)
        lag_s = lag_in * (active_last - col - 1)
        steps = n_in + lag_in * (n_col - 2)
        for i in range(steps):
            c_p = i - lag_p
            c_s = i - lag_s

            @pl.when(jnp.logical_and(within(c_p, 0, n_in), jnp.logical_and(col > 0, col <= active_last)))
            def _():
                i_up(s, it, c_p, i_own.at[it, s, c_p]).wait_recv()

                @pl.when(col < active_last)
                def _():
                    i_put_p[it, s, c_p] = i_got_p[it, s, c_p] + i_own[it, s, c_p]
                    i_up(s, it, c_p, i_put_p.at[it, s, c_p]).start()

            @pl.when(jnp.logical_and(within(c_s, 0, n_in), col < active_last))
            def _():
                i_down(s, it, c_s, i_own.at[it, s, c_s]).wait_recv()

                @pl.when(col > 0)
                def _():
                    i_put_s[it, s, c_s] = i_got_s[it, s, c_s] + i_own[it, s, c_s]
                    i_down(s, it, c_s, i_put_s.at[it, s, c_s]).start()
            if i < steps - 1:
                yield 0.05, 2.2 / lag_in

        @pl.when(col <= active_last)
        def _():
            inner = []
            for c in range(n_in):
                before = jnp.where(is_first, 0.0, i_got_p[it, s, c])
                after = jnp.where(col == active_last, 0.0, i_got_s[it, s, c])
                inner.append(before + i_own[it, s, c] + after)
            acc[s] = product(stacked(jnp.concatenate(inner, axis=0)), r_hi[...], r_lo[...], NT)

        @pl.when(col > active_last)
        def _():
            acc[s] = jnp.zeros_like(acc[s])

    def drain_solve(s, it):
        for c in range(n_in):
            @pl.when(col < active_last)
            def _():
                i_up(s, it, c, i_own.at[it, s, c]).wait_send()

            @pl.when(jnp.logical_and(col > 0, col <= active_last))
            def _():
                i_down(s, it, c, i_own.at[it, s, c]).wait_send()

    total_q = n_col * n_half

    def f_up(s, q, src):
        b = n_col - 1 - q // n_half
        return line(src, f_got_p.at[s, b, lax.rem(q, n_half)], f_sem.at[s], 0, q, 1)

    def f_down(s, q, src):
        b = q // n_half
        return line(src, f_got_s.at[s, b, lax.rem(q, n_half)], f_sem.at[s], 1, q, -1)

    def finish(s):
        f_cat = stacked(field[s])
        per = width // rows_c
        for c in range(chunks):
            value = fit(s, c, f_cat)
            for b in range(n_col):
                f_own[s, b, c // per, :, (c % per) * rows_c:(c % per + 1) * rows_c] = value[b * sub:(b + 1) * sub, :]
            if c < chunks - 1:
                yield COST_FIT, 0.0

        @pl.when(is_first)
        def _():
            for q in range(total_q - n_half):
                f_up(s, q, f_own.at[s, n_col - 1 - q // n_half, q % n_half]).start()

        @pl.when(is_last)
        def _():
            for q in range(total_q - n_half):
                f_down(s, q, f_own.at[s, q // n_half, q % n_half]).start()
        yield COST_FIT, 2.4
        lag_p = lag_f * (col - 1)
        lag_s = lag_f * (n_col - 2 - col)
        steps = max(total_q - z * n_half + lag_f * (z - 1) for z in range(1, n_col))
        for i in range(steps):
            q_p = i - lag_p
            q_s = i - lag_s
            b_p = n_col - 1 - q_p // n_half
            b_s = q_s // n_half

            @pl.when(jnp.logical_and(within(q_p, 0, total_q - col * n_half), col > 0))
            def _():
                h_p = lax.rem(q_p, n_half)
                f_up(s, q_p, f_own.at[s, b_p, h_p]).wait_recv()

                @pl.when(b_p > col)
                def _():
                    f_put_p[s, b_p, h_p] = f_got_p[s, b_p, h_p] + f_own[s, b_p, h_p]
                    f_up(s, q_p, f_put_p.at[s, b_p, h_p]).start()

            @pl.when(jnp.logical_and(within(q_s, 0, (col + 1) * n_half), col < n_col - 1))
            def _():
                h_s = lax.rem(q_s, n_half)
                f_down(s, q_s, f_own.at[s, b_s, h_s]).wait_recv()

                @pl.when(b_s < col)
                def _():
                    f_put_s[s, b_s, h_s] = f_got_s[s, b_s, h_s] + f_own[s, b_s, h_s]
                    f_down(s, q_s, f_put_s.at[s, b_s, h_s]).start()
            yield 0.1, PITCH
        for h in range(n_half):
            before = jnp.where(is_first, 0.0, f_got_p[s, col, h])
            after = jnp.where(is_last, 0.0, f_got_s[s, col, h])
            residual[s * sub:(s + 1) * sub, h * width:(h + 1) * width] = -(before + f_own[s, col, h] + after)

    def drain_finish(s):
        def drain(q, carry):
            @pl.when(q < (n_col - 1 - col) * n_half)
            def _():
                f_up(s, q, f_own.at[s, 0, 0]).wait_send()

            @pl.when(q < col * n_half)
            def _():
                f_down(s, q, f_own.at[s, 0, 0]).wait_send()
            return carry

        lax.fori_loop(0, total_q, drain, 0)

    def stream(s):
        for it in range(ITERS):
            yield from fit_and_sum(s, it)
            yield from row_sum(s, 2 * it)
            yield from solve(s, it)
            yield from row_sum(s, 2 * it + 1)
            change = acc[s]
            field[s] = field[s] - change
            if it == 0:
                total_change[s] = -change
            else:
                for b in range(n_col):
                    at = b * blk + s * sub
                    correction[at:at + sub, :] = total_change[s, b * sub:(b + 1) * sub, :] - change[b * sub:(b + 1) * sub]
        yield from finish(s)

    work = [[0.001 * s, s, stream(s)] for s in range(streams)]
    now = 0.0
    while work:
        work.sort(key=lambda entry: entry[:2])
        entry = work[0]
        now = max(now, entry[0])
        step = next(entry[2], None)
        if step is None:
            work.remove(entry)
            continue
        now += step[0]
        entry[0] = now + step[1]

    for copy in sent:
        copy.wait_send()
    for s in range(streams):
        for it in range(ITERS):
            drain_sum(s, it)
            drain_solve(s, it)
        drain_finish(s)


def local(n_row, n_col, dosage, phenotypes, solution, inverse_factor):
    rows, cols = dosage.shape
    blk = phenotypes.shape[1]
    n_rb = inverse_factor.shape[1]
    streams = 2
    n_all = solution.shape[1]
    n_p = n_all // streams
    chunks = 8
    rows_c = rows // chunks
    n_in = 2
    n_half = 2
    n_x = n_row // 2
    lags = (3, 2, 3) if n_col <= 4 else (1, 1, 1)
    big = pltpu.VMEM((ITERS, streams, chunks, n_p, rows_c), F32)
    last = pltpu.VMEM((streams, n_col, n_half, blk // streams, rows // n_half), F32)
    mid = pltpu.VMEM((ITERS, streams, n_in, n_p // n_in, n_rb), F32)
    vec = pltpu.VMEM((streams, n_p, cols), F32)
    k = 2 * ITERS
    scratch = [
        pltpu.VMEM((chunks, rows_c, cols), F32),
        pltpu.VMEM((chunks, rows_c, cols), BF16),
        pltpu.VMEM((chunks, rows_c, cols), BF16),
        pltpu.VMEM((blk, rows), F32),
        pltpu.VMEM((streams, chunks, n_p, rows_c), F32),
        pltpu.VMEM((n_all, cols), F32),
        vec, vec,
        pltpu.VMEM(inverse_factor.shape, F32),
        pltpu.VMEM(inverse_factor.shape, BF16),
        pltpu.VMEM(inverse_factor.shape, BF16),
        big, big, big, big, big,
        last, last, last, last, last,
        vec,
        pltpu.VMEM((k, streams, n_p // 2, cols), F32),
        pltpu.VMEM((k, streams, n_p // 2, cols), F32),
        pltpu.VMEM((k, streams, max(n_x - 1, 1), n_p // 2, cols), F32),
        pltpu.VMEM((k, streams, 2, n_p // 2, cols), F32),
        pltpu.VMEM((k, streams, 3, n_p // 2, cols), F32),
        mid, mid, mid, mid, mid,
        pltpu.SemaphoreType.DMA((3,)),
        pltpu.SemaphoreType.DMA((chunks,)),
        pltpu.SemaphoreType.DMA((ITERS, streams, 2, 2, chunks)),
        pltpu.SemaphoreType.DMA((streams, 2, 2, n_col * n_half)),
        pltpu.SemaphoreType.DMA((k, streams, 4)),
        pltpu.SemaphoreType.DMA((k, streams, max(n_x - 1, 1))),
        pltpu.SemaphoreType.DMA((k, streams, max(n_x - 1, 1))),
        pltpu.SemaphoreType.DMA((ITERS, streams, 2, 2, n_in)),
    ]
    any_spec = pl.BlockSpec(memory_space=pl.ANY)
    vmem_spec = pl.BlockSpec(memory_space=pltpu.VMEM)
    residual, correction = pl.pallas_call(
        functools.partial(kernel, (n_row, n_col, streams, chunks, n_in, *lags)),
        out_shape=(
            jax.ShapeDtypeStruct((blk, rows), F32),
            jax.ShapeDtypeStruct((n_all, cols), F32),
        ),
        in_specs=[any_spec] * 4,
        out_specs=(vmem_spec, vmem_spec),
        scratch_shapes=scratch,
        compiler_params=pltpu.CompilerParams(collective_id=0, has_side_effects=True),
    )(dosage, phenotypes.T, solution.T, inverse_factor)
    return residual.T, correction.T


def solution(mesh):
    return jax.shard_map(
        functools.partial(local, mesh.shape["row"], mesh.shape["col"]),
        mesh=mesh,
        in_specs=(
            P(("grp", "row"), "col"),
            P(("grp", "row"), "col"),
            P(("grp", "col"), None),
            P(("grp", "col"), "row"),
        ),
        out_specs=(P(("grp", "row"), "col"), P(("grp", "col"), None)),
        check_vma=False,
    )
```

```python
import functools

import jax
import jax.numpy as jnp
from jax import lax
from jax.experimental import pallas as pl
from jax.experimental.pallas import tpu as pltpu
from jax.sharding import PartitionSpec as P

ITERS = 2
MESH = pl.DeviceIdType.MESH
F32 = jnp.float32
BF16 = jnp.bfloat16
NN = (((1,), (0,)), ((), ()))
NT = (((1,), (1,)), ((), ()))


def split(value):
    high = value.astype(BF16)
    low = (value - high.astype(F32)).astype(BF16)
    return high, low


def product(left, right_high, right_low, dims):
    count = left.shape[0] // 2
    main = lax.dot_general(left, right_high, dims, preferred_element_type=F32)
    rest = lax.dot_general(left[:count], right_low, dims, preferred_element_type=F32)
    return main[:count] + (main[count:] + rest)


def stacked(value):
    return jnp.concatenate(split(value), axis=0)


def kernel(cfg, dosage, pheno, start, factor, residual, correction, *scratch):
    (n_row, n_col, chunks, n_in) = cfg
    (d_f32, d_hi, d_lo, y_in, y_pad, f_in, field, r_f32, r_hi, r_lo,
     own, got_p, got_s, put_p, put_s,
     f_own, f_got_p, f_got_s, f_put_p, f_put_s,
     acc, pair_got, cross_put, cross_got, back_put, back_got,
     i_own, i_got_p, i_got_s, i_put_p, i_put_s, inner,
     load_sem, d_sem, a_sem, f_sem, pair_sem, cross_ssem, cross_rsem, i_sem) = scratch
    rows_c = d_hi.shape[1]
    n_p = field.shape[0]
    half = n_p // 2
    blk = pheno.shape[0]
    n_half = f_own.shape[1]
    width = f_own.shape[3]
    n_x = n_row // 2

    row = lax.axis_index("row")
    col = lax.axis_index("col")
    core = lax.rem(row, 2)
    x = row // 2
    partner = {"row": row + 1 - 2 * core}
    is_first = col == 0
    is_last = col == n_col - 1

    loads = []
    for k, (src, dst) in enumerate(((start, f_in), (pheno, y_in), (factor, r_f32))):
        loads.append(pltpu.make_async_copy(src, dst, load_sem.at[k]))

    def d_copy(c):
        return pltpu.make_async_copy(
            dosage.at[pl.ds(pl.multiple_of(c * rows_c, rows_c), rows_c), :], d_f32.at[c], d_sem.at[c])

    loads[0].start()
    loads[1].start()
    for c in range(chunks):
        d_copy(c).start()
    loads[2].start()

    barrier = pltpu.get_barrier_semaphore()

    @pl.when(col > 0)
    def _():
        pl.semaphore_signal(barrier, inc=1, device_id={"col": col - 1}, device_id_type=MESH)

    @pl.when(col < n_col - 1)
    def _():
        pl.semaphore_signal(barrier, inc=1, device_id={"col": col + 1}, device_id_type=MESH)

    pl.semaphore_signal(barrier, inc=1, device_id=partner, device_id_type=MESH)
    for d in range(1, n_x):
        other = lax.rem(x + d, n_x) * 2 + core
        pl.semaphore_signal(barrier, inc=1, device_id={"row": other}, device_id_type=MESH)

    loads[0].wait()
    loads[1].wait()
    field[...] = f_in[...]
    for c in range(chunks):
        y_c = y_in[:, c * rows_c:(c + 1) * rows_c]
        for b in range(n_col):
            y_pad[c, b * blk:(b + 1) * blk, :] = jnp.where(col == b, y_c, 0.0)

    up_down = jnp.where(is_first, 0, 1) + jnp.where(is_last, 0, 1)
    pl.semaphore_wait(barrier, n_x + up_down)

    def line(src, dst, sems, way, c, step):
        return pltpu.make_async_remote_copy(
            src_ref=src, dst_ref=dst, send_sem=sems.at[way, 0, c], recv_sem=sems.at[way, 1, c],
            device_id={"col": jnp.clip(col + step, 0, n_col - 1)}, device_id_type=MESH)

    def fit(c, f_cat):
        return product(f_cat, d_hi[c], d_lo[c], NT) - y_pad[c]

    def up(it, c, src):
        return line(src, got_p.at[it, c], a_sem.at[it], 0, c, 1)

    def down(it, c, src):
        return line(src, got_s.at[it, c], a_sem.at[it], 1, c, -1)

    def fit_and_sum(it):
        f_cat = stacked(field[...])

        def make(c, carry):
            if it == 0:
                d_copy(c).wait()
                high, low = split(d_f32[c])
                d_hi[c] = high
                d_lo[c] = low
            own[it, c] = fit(c, f_cat)

            @pl.when(is_first)
            def _():
                up(it, c, own.at[it, c]).start()

            @pl.when(is_last)
            def _():
                down(it, c, own.at[it, c]).start()
            return carry

        lax.fori_loop(0, chunks, make, 0)
        acc[...] = jnp.zeros_like(acc)
        middle = jnp.logical_and(col > 0, col < n_col - 1)
        lag = jnp.where(middle, 4 * (n_col - 1 - 2 * col), 0)
        lag_s = jnp.clip(lag, 0, chunks)
        lag_p = jnp.clip(-lag, 0, chunks)
        lag_max = min(chunks, 4 * max(n_col - 3, 0))

        def step(i, carry):
            c_p = i - lag_p
            c_s = i - lag_s

            @pl.when(jnp.logical_and(jnp.logical_and(c_p >= 0, c_p < chunks), col > 0))
            def _():
                up(it, c_p, own.at[it, c_p]).wait_recv()

                @pl.when(col < n_col - 1)
                def _():
                    put_p[it, c_p] = got_p[it, c_p] + own[it, c_p]
                    up(it, c_p, put_p.at[it, c_p]).start()

            @pl.when(jnp.logical_and(jnp.logical_and(c_s >= 0, c_s < chunks), col < n_col - 1))
            def _():
                down(it, c_s, own.at[it, c_s]).wait_recv()

                @pl.when(col > 0)
                def _():
                    put_s[it, c_s] = got_s[it, c_s] + own[it, c_s]
                    down(it, c_s, put_s.at[it, c_s]).start()

            c = i - lag_p - lag_s

            @pl.when(jnp.logical_and(c >= 0, c < chunks))
            def _():
                before = jnp.where(is_first, 0.0, got_p[it, c])
                after = jnp.where(is_last, 0.0, got_s[it, c])
                resid = before + own[it, c] + after
                acc[...] += product(stacked(resid), d_hi[c], d_lo[c], NN)
            return carry

        lax.fori_loop(0, chunks + lag_max, step, 0)

    def drain_sum(it):
        def step(c, carry):
            @pl.when(col < n_col - 1)
            def _():
                up(it, c, own.at[it, c]).wait_send()

            @pl.when(col > 0)
            def _():
                down(it, c, own.at[it, c]).wait_send()
            return carry

        lax.fori_loop(0, chunks, step, 0)

    def row_sum(k):
        for h in range(2):
            back_put[k, h] = acc[h * half:(h + 1) * half, :]
        first = pltpu.make_async_remote_copy(
            src_ref=back_put.at[k, 1 - core], dst_ref=pair_got.at[k],
            send_sem=pair_sem.at[k, 0], recv_sem=pair_sem.at[k, 1],
            device_id=partner, device_id_type=MESH)
        first.start()
        first.wait_recv()
        cross_put[k] = back_put[k, core] + pair_got[k]
        sends = []
        for d in range(1, n_x):
            other = lax.rem(x + d, n_x) * 2 + core
            sends.append(pltpu.make_async_remote_copy(
                src_ref=cross_put.at[k], dst_ref=cross_got.at[k, d - 1],
                send_sem=cross_ssem.at[k, d - 1], recv_sem=cross_rsem.at[k, d - 1],
                device_id={"row": other}, device_id_type=MESH))
            sends[-1].start()
        parts = [cross_put[k]]
        for d in range(1, n_x):
            sends[d - 1].wait_recv()
            parts.append(cross_got[k, d - 1])
        total = None
        for chip in range(n_x):
            here = parts[0]
            for d in range(1, n_x):
                here = jnp.where(lax.rem(x - d + n_x, n_x) == chip, parts[d], here)
            total = here if total is None else total + here
        back_got[k, 2] = total
        last = pltpu.make_async_remote_copy(
            src_ref=back_got.at[k, 2], dst_ref=back_got.at[k, core],
            send_sem=pair_sem.at[k, 2], recv_sem=pair_sem.at[k, 3],
            device_id=partner, device_id_type=MESH)
        last.start()
        last.wait_recv()
        theirs = back_got[k, 1 - core]
        mine = total
        low = jnp.where(core == 0, mine, theirs)
        high = jnp.where(core == 0, theirs, mine)
        acc[0:half, :] = low
        acc[half:, :] = high
        for copy in (first, last, *sends):
            copy.wait_send()

    n_rb = r_hi.shape[1]
    n_cb = r_hi.shape[0]
    active_last = ((row + 1) * n_rb + n_cb - 1) // n_cb - 1
    active_last = jnp.minimum(active_last, n_col - 1)
    wide_i = n_p // n_in

    def i_up(it, c, src):
        return line(src, i_got_p.at[it, c], i_sem.at[it], 0, c, 1)

    def i_down(it, c, src):
        return line(src, i_got_s.at[it, c], i_sem.at[it], 1, c, -1)

    def solve(it):
        if it == 0:
            loads[2].wait()
            high, low = split(r_f32[...])
            r_hi[...] = high
            r_lo[...] = low

        @pl.when(col <= active_last)
        def _():
            part = product(stacked(acc[...]), r_hi[...], r_lo[...], NN)
            for c in range(n_in):
                i_own[it, c] = part[c * wide_i:(c + 1) * wide_i]

            @pl.when(jnp.logical_and(is_first, active_last > 0))
            def _():
                for c in range(n_in):
                    i_up(it, c, i_own.at[it, c]).start()

            @pl.when(jnp.logical_and(col == active_last, active_last > 0))
            def _():
                for c in range(n_in):
                    i_down(it, c, i_own.at[it, c]).start()

            lag = jnp.where(jnp.logical_and(col > 0, col < active_last), 2 * (active_last - 2 * col), 0)
            lag_s = jnp.clip(lag, 0, n_in)
            lag_p = jnp.clip(-lag, 0, n_in)
            lag_max = min(n_in, 2 * max(n_col - 3, 0))

            def step(i, carry):
                c_p = i - lag_p
                c_s = i - lag_s

                @pl.when(jnp.logical_and(jnp.logical_and(c_p >= 0, c_p < n_in), col > 0))
                def _():
                    i_up(it, c_p, i_own.at[it, c_p]).wait_recv()

                    @pl.when(col < active_last)
                    def _():
                        i_put_p[it, c_p] = i_got_p[it, c_p] + i_own[it, c_p]
                        i_up(it, c_p, i_put_p.at[it, c_p]).start()

                @pl.when(jnp.logical_and(jnp.logical_and(c_s >= 0, c_s < n_in), col < active_last))
                def _():
                    i_down(it, c_s, i_own.at[it, c_s]).wait_recv()

                    @pl.when(col > 0)
                    def _():
                        i_put_s[it, c_s] = i_got_s[it, c_s] + i_own[it, c_s]
                        i_down(it, c_s, i_put_s.at[it, c_s]).start()
                return carry

            lax.fori_loop(0, n_in + lag_max, step, 0)
            for c in range(n_in):
                before = jnp.where(is_first, 0.0, i_got_p[it, c])
                after = jnp.where(col == active_last, 0.0, i_got_s[it, c])
                inner[c * wide_i:(c + 1) * wide_i, :] = before + i_own[it, c] + after
            acc[...] = product(stacked(inner[...]), r_hi[...], r_lo[...], NT)

        @pl.when(col > active_last)
        def _():
            acc[...] = jnp.zeros_like(acc)

    def drain_solve(it):
        for c in range(n_in):
            @pl.when(col < active_last)
            def _():
                i_up(it, c, i_own.at[it, c]).wait_send()

            @pl.when(jnp.logical_and(col > 0, col <= active_last))
            def _():
                i_down(it, c, i_own.at[it, c]).wait_send()

    def f_up(q, src):
        b = n_col - 1 - q // n_half
        return line(src, f_got_p.at[b, lax.rem(q, n_half)], f_sem, 0, q, 1)

    def f_down(q, src):
        b = q // n_half
        return line(src, f_got_s.at[b, lax.rem(q, n_half)], f_sem, 1, q, -1)

    def finish():
        f_cat = stacked(field[...])
        per = width // rows_c
        for c in range(chunks):
            value = fit(c, f_cat)
            for b in range(n_col):
                f_own[b, c // per, :, (c % per) * rows_c:(c % per + 1) * rows_c] = value[b * blk:(b + 1) * blk, :]
        total_q = n_col * n_half

        @pl.when(is_first)
        def _():
            def send(q, carry):
                f_up(q, f_own.at[n_col - 1 - q // n_half, lax.rem(q, n_half)]).start()
                return carry
            lax.fori_loop(0, total_q - n_half, send, 0)

        @pl.when(is_last)
        def _():
            def send(q, carry):
                f_down(q, f_own.at[q // n_half, lax.rem(q, n_half)]).start()
                return carry
            lax.fori_loop(0, total_q - n_half, send, 0)

        middle = jnp.logical_and(col > 0, col < n_col - 1)
        lag = jnp.where(middle, 4 * (n_col - 1 - 2 * col), 0)
        lag_s = jnp.clip(lag, 0, total_q)
        lag_p = jnp.clip(-lag, 0, total_q)
        lag_max = min(total_q, 4 * max(n_col - 3, 0))

        def step(i, carry):
            q_p = i - lag_p
            q_s = i - lag_s
            b_p = n_col - 1 - q_p // n_half
            h_p = lax.rem(q_p, n_half)
            b_s = q_s // n_half
            h_s = lax.rem(q_s, n_half)

            @pl.when(jnp.logical_and(jnp.logical_and(q_p >= 0, q_p < total_q - col * n_half), col > 0))
            def _():
                f_up(q_p, f_own.at[b_p, h_p]).wait_recv()

                @pl.when(b_p > col)
                def _():
                    f_put_p[b_p, h_p] = f_got_p[b_p, h_p] + f_own[b_p, h_p]
                    f_up(q_p, f_put_p.at[b_p, h_p]).start()

            @pl.when(jnp.logical_and(jnp.logical_and(q_s >= 0, q_s < (col + 1) * n_half), col < n_col - 1))
            def _():
                f_down(q_s, f_own.at[b_s, h_s]).wait_recv()

                @pl.when(b_s < col)
                def _():
                    f_put_s[b_s, h_s] = f_got_s[b_s, h_s] + f_own[b_s, h_s]
                    f_down(q_s, f_put_s.at[b_s, h_s]).start()
            return carry

        lax.fori_loop(0, total_q + lag_max, step, 0)
        for h in range(n_half):
            before = jnp.where(is_first, 0.0, f_got_p[col, h])
            after = jnp.where(is_last, 0.0, f_got_s[col, h])
            residual[:, h * width:(h + 1) * width] = -(before + f_own[col, h] + after)

        def drain(q, carry):
            @pl.when(q < (n_col - 1 - col) * n_half)
            def _():
                f_up(q, f_own.at[0, 0]).wait_send()

            @pl.when(q < col * n_half)
            def _():
                f_down(q, f_own.at[0, 0]).wait_send()
            return carry

        lax.fori_loop(0, total_q, drain, 0)

    for it in range(ITERS):
        fit_and_sum(it)
        row_sum(2 * it)
        solve(it)
        row_sum(2 * it + 1)
        field[...] = field[...] - acc[...]
        if it == 0:
            correction[...] = -acc[...]
        else:
            correction[...] = correction[...] - acc[...]
    finish()
    for it in range(ITERS):
        drain_sum(it)
        drain_solve(it)


def local(n_row, n_col, dosage, phenotypes, solution, inverse_factor):
    rows, cols = dosage.shape
    blk = phenotypes.shape[1]
    n_p = solution.shape[1]
    n_rb = inverse_factor.shape[1]
    chunks = 16
    rows_c = rows // chunks
    n_in = 4
    n_half = 4
    n_x = n_row // 2
    big = pltpu.VMEM((ITERS, chunks, n_p, rows_c), F32)
    last = pltpu.VMEM((n_col, n_half, blk, rows // n_half), F32)
    mid = pltpu.VMEM((ITERS, n_in, n_p // n_in, n_rb), F32)
    k = 2 * ITERS
    scratch = [
        pltpu.VMEM((chunks, rows_c, cols), F32),
        pltpu.VMEM((chunks, rows_c, cols), BF16),
        pltpu.VMEM((chunks, rows_c, cols), BF16),
        pltpu.VMEM((blk, rows), F32),
        pltpu.VMEM((chunks, n_p, rows_c), F32),
        pltpu.VMEM((n_p, cols), F32),
        pltpu.VMEM((n_p, cols), F32),
        pltpu.VMEM(inverse_factor.shape, F32),
        pltpu.VMEM(inverse_factor.shape, BF16),
        pltpu.VMEM(inverse_factor.shape, BF16),
        big, big, big, big, big,
        last, last, last, last, last,
        pltpu.VMEM((n_p, cols), F32),
        pltpu.VMEM((k, n_p // 2, cols), F32),
        pltpu.VMEM((k, n_p // 2, cols), F32),
        pltpu.VMEM((k, max(n_x - 1, 1), n_p // 2, cols), F32),
        pltpu.VMEM((k, 2, n_p // 2, cols), F32),
        pltpu.VMEM((k, 3, n_p // 2, cols), F32),
        mid, mid, mid, mid, mid,
        pltpu.VMEM((n_p, n_rb), F32),
        pltpu.SemaphoreType.DMA((3,)),
        pltpu.SemaphoreType.DMA((chunks,)),
        pltpu.SemaphoreType.DMA((ITERS, 2, 2, chunks)),
        pltpu.SemaphoreType.DMA((2, 2, n_col * n_half)),
        pltpu.SemaphoreType.DMA((k, 4)),
        pltpu.SemaphoreType.DMA((k, max(n_x - 1, 1))),
        pltpu.SemaphoreType.DMA((k, max(n_x - 1, 1))),
        pltpu.SemaphoreType.DMA((ITERS, 2, 2, n_in)),
    ]
    any_spec = pl.BlockSpec(memory_space=pl.ANY)
    vmem_spec = pl.BlockSpec(memory_space=pltpu.VMEM)
    residual, correction = pl.pallas_call(
        functools.partial(kernel, (n_row, n_col, chunks, n_in)),
        out_shape=(
            jax.ShapeDtypeStruct((blk, rows), F32),
            jax.ShapeDtypeStruct((n_p, cols), F32),
        ),
        in_specs=[any_spec] * 4,
        out_specs=(vmem_spec, vmem_spec),
        scratch_shapes=scratch,
        compiler_params=pltpu.CompilerParams(collective_id=0, has_side_effects=True),
    )(dosage, phenotypes.T, solution.T, inverse_factor)
    return residual.T, correction.T


def solution(mesh):
    return jax.shard_map(
        functools.partial(local, mesh.shape["row"], mesh.shape["col"]),
        mesh=mesh,
        in_specs=(
            P(("grp", "row"), "col"),
            P(("grp", "row"), "col"),
            P(("grp", "col"), None),
            P(("grp", "col"), "row"),
        ),
        out_specs=(P(("grp", "row"), "col"), P(("grp", "col"), None)),
        check_vma=False,
    )
```
